32 devices in a mesh: cfg: 2 (over y), row: 4 (over z), col: 2 (over x), spin: 2 (over core).
Axes of the slice: x: 2, y: 2, z: 4, core: 2. Of those that a mesh axis runs over, the one named last changes fastest.
Arguments:
- perambulator: float32 [2, 8192, 4096], P(None, ('cfg', 'row'), ('col', 'spin')), parts along dimension 1, may hold values from -1 to 1
- insertion_ops: float32 [2, 2, 64, 64], replicated, may hold values from -0.75 to 0.75
- ins_times: int32 [2], replicated, may hold values from 0 to 15
- sign_table: int32 [2, 4], replicated, may hold values from 0 to 3
- perm_table: int32 [2, 4], replicated, may hold values from 0 to 3, each once within a row
Outputs:
- generalized: float32 [2, 8192, 4096], P(None, ('cfg', 'row'), ('col', 'spin')), parts along dimension 1
The draws below stay inside these ranges and needn't reach their ends.
There are 2 independent parts, one for each index of `cfg`. The reference program is written for one: setup_inputs(seed, part) draws one part's arguments, and reference() takes and returns one part's arrays. A program takes and returns all parts, laid end to end along the dimension named above; an argument that names none is the same for every part. Nothing has to cross between parts.
All inputs are finite; a program needn't handle non-finite values.
Results may differ from the reference program's by a relative error of at most 0.0001.
Values sent between devices are 32-bit elements; how exact they have to be, the bound alone decides.
A program may use at most 64 MiB of HBM per device.

```python
import jax
import jax.numpy as jnp
from jax import lax

NV = 64
NS = 4
B = 256
NT = 16
NINS = 2


def set_ends(values, own_key, least, largest):
    longest = values.shape.index(max(values.shape))
    spots = []
    for shift in (0, 1):
        where = [jax.random.randint(jax.random.fold_in(own_key, axis), (), 0, length) for axis, length in enumerate(values.shape)]
        where[longest] = (where[longest] + shift) % values.shape[longest]
        spots.append(tuple(where))
    return values.at[spots[0]].set(least).at[spots[1]].set(largest)


def block_scale(rng, shape, cuts, smallest, largest):
    gain, own = 1.0, jax.random.fold_in(rng, 6)
    for dim, blocks in cuts:
        heights = jnp.exp(jax.random.uniform(jax.random.fold_in(own, dim), (blocks,), jnp.float32, smallest / len(cuts), largest / len(cuts)))
        gain = gain * jnp.repeat(heights, shape[dim] // blocks).reshape([-1 if axis == dim else 1 for axis in range(len(shape))])
    return gain


def noise(rng, shape, spread, reach, cuts=(), held_as=jnp.bfloat16):
    gain = block_scale(rng, shape, cuts, -0.22, 0.18) if cuts else 1.0
    values = jax.random.normal(rng, shape, jnp.float32) * spread * gain
    return jnp.minimum(jnp.maximum(values, -reach), reach).astype(held_as)


def setup_inputs(seed: int = 0, part: int = 0) -> dict:
    keys = jax.random.split(jax.random.key(seed), 6)
    own_keys = jax.random.split(jax.random.fold_in(keys[5], part), 6)
    return {
        "perambulator": noise(own_keys[0], (2, NT * B, NT * B), 0.125, 1.0, ((1, 4), (2, 4)), jnp.float32),
        "insertion_ops": noise(keys[1], (NINS, 2, NV, NV), NV ** -0.5, 0.75, (), jnp.float32),
        "ins_times": jax.random.randint(keys[2], (NINS,), 0, NT).astype(jnp.int32),
        "sign_table": set_ends(jax.random.randint(keys[3], (NINS, NS), 0, 4), jax.random.fold_in(keys[3], 1), 0, 3).astype(jnp.int32),
        "perm_table": jax.vmap(lambda own: jax.random.permutation(own, NS))(jax.random.split(keys[4], NINS)).reshape((NINS, NS)).astype(jnp.int32),
    }


def complex_dot(former_real, former_imag, latter_real, latter_imag):
    maximal_precision = lax.Precision.HIGHEST
    real_part = jnp.dot(former_real, latter_real, precision=maximal_precision) - jnp.dot(former_imag, latter_imag, precision=maximal_precision)
    imag_part = jnp.dot(former_real, latter_imag, precision=maximal_precision) + jnp.dot(former_imag, latter_real, precision=maximal_precision)
    return real_part, imag_part


def insert_current_operator(row_slab, op_real, op_imag, sign_row, perm_row):
    maximal_precision = lax.Precision.HIGHEST
    col_count = row_slab.shape[2]
    slab_real = row_slab[0].reshape(NS, NV, col_count)
    slab_imag = row_slab[1].reshape(NS, NV, col_count)
    combined_real = jnp.einsum("ab,sbc->sac", op_real, slab_real, precision=maximal_precision) - jnp.einsum("ab,sbc->sac", op_imag, slab_imag, precision=maximal_precision)
    combined_imaginary = jnp.einsum("ab,sbc->sac", op_real, slab_imag, precision=maximal_precision) + jnp.einsum("ab,sbc->sac", op_imag, slab_real, precision=maximal_precision)
    selected_real = combined_real[perm_row]
    selected_imaginary = combined_imaginary[perm_row]
    phase_factor_real = jnp.array([1.0, 0.0, -1.0, 0.0], jnp.float32)[sign_row][:, None, None]
    phase_imag = jnp.array([0.0, 1.0, 0.0, -1.0], jnp.float32)[sign_row][:, None, None]
    out_real = phase_factor_real * selected_real - phase_imag * selected_imaginary
    out_imag = phase_factor_real * selected_imaginary + phase_imag * selected_real
    return out_real.reshape(B, col_count), out_imag.reshape(B, col_count)


def reference(perambulator, insertion_ops, ins_times, sign_table, perm_table):
    size_all = NT * B
    total_real = jnp.zeros((size_all, size_all), jnp.float32)
    total_imag = jnp.zeros((size_all, size_all), jnp.float32)
    for ins_index in range(NINS):
        start_row = (ins_times[ins_index] * B).astype(jnp.int32)
        row_slab = lax.dynamic_slice_in_dim(perambulator, start_row, B, 1)
        col_slab = lax.dynamic_slice_in_dim(perambulator, start_row, B, 2)
        inserted_real, inserted_imag = insert_current_operator(row_slab, insertion_ops[ins_index, 0], insertion_ops[ins_index, 1], sign_table[ins_index], perm_table[ins_index])
        part_real, part_imag = complex_dot(col_slab[0], col_slab[1], inserted_real, inserted_imag)
        total_real = total_real + part_real
        total_imag = total_imag + part_imag
    return jnp.stack([total_real, total_imag])
```

```python
import functools

import jax
import jax.numpy as jnp
from jax import lax
from jax.experimental import pallas as pl
from jax.experimental.pallas import tpu as pltpu
from jax.sharding import PartitionSpec as P

MESH = pl.DeviceIdType.MESH
WIDTH = 128
SKEW = 2
PACE = 2


def split(value):
    high = value.astype(jnp.bfloat16)
    low = (value - high.astype(jnp.float32)).astype(jnp.bfloat16)
    return high, low


def kernel(
    sizes,
    rc, lc, amat, out,
    fl, fr, ph, xown, xl, xr, lfin, lhi, llo, bhi, blo, stage,
    zs, zr, xs, xrs, ps, pr, ls, lr, os,
):
    nz, nx, kcount, order, rows, groups, per_group, lchunks, lrows = sizes
    chunks = groups * per_group
    z = lax.axis_index("row")
    x = lax.axis_index("col")
    h = lax.axis_index("spin")
    other = 1 - h
    barrier = pltpu.get_barrier_semaphore()

    for pos, n, axis in ((z, nz, "row"), (x, nx, "col")):
        @pl.when(pos > 0)
        def _():
            pl.semaphore_signal(barrier, inc=1, device_id={axis: (pos + n - 1) % n}, device_id_type=MESH)

        @pl.when(pos < n - 1)
        def _():
            pl.semaphore_signal(barrier, inc=1, device_id={axis: (pos + 1) % n}, device_id_type=MESH)
    pl.semaphore_signal(barrier, inc=1, device_id={"spin": other}, device_id_type=MESH)
    ends = [jnp.where(pos == end, 1, 0) for pos, n in ((z, nz), (x, nx)) for end in (0, n - 1)]
    pl.semaphore_wait(barrier, 5 - sum(ends))

    def hop(buf, c, send, recv, side, pos, n, axis):
        to = (pos + 1) % n if side == 0 else (pos + n - 1) % n
        return pltpu.make_async_remote_copy(
            src_ref=buf.at[c], dst_ref=buf.at[c],
            send_sem=send.at[side, c], recv_sem=recv.at[side, c],
            device_id={axis: to}, device_id_type=MESH,
        )

    def half_copy(c):
        return pltpu.make_async_remote_copy(
            src_ref=lc.at[other, c], dst_ref=ph.at[c],
            send_sem=ps.at[c], recv_sem=pr.at[c],
            device_id={"spin": other}, device_id_type=MESH,
        )

    def final_copy(c):
        return pltpu.make_async_remote_copy(
            src_ref=lfin.at[h, c], dst_ref=lfin.at[h, c],
            send_sem=ls.at[c], recv_sem=lr.at[c],
            device_id={"spin": other}, device_id_type=MESH,
        )

    flows = (
        (fl, rc, zs, zr, 0, z, nz, "row", chunks),
        (fr, rc, zs, zr, 1, z, nz, "row", chunks),
        (xl, xown, xs, xrs, 0, x, nx, "col", lchunks),
        (xr, xown, xs, xrs, 1, x, nx, "col", lchunks),
    )

    @pl.loop(0, lchunks)
    def _(c):
        half_copy(c).start()

    def step(s):
        @pl.when(s < lchunks)
        def _():
            half_copy(s).wait_recv()
            xown[s] = lc[h, s] + ph[s]

        for buf, own, send, recv, side, pos, n, axis, count in flows:
            far = pos if side == 0 else n - 1 - pos
            c = s - SKEW * far
            live = (c >= 0) & (c < count)

            @pl.when(live & (far > 0))
            def _():
                hop(buf, c, send, recv, side, pos, n, axis).wait_recv()
                buf[c] = buf[c] + own[c]

            @pl.when(live & (far == 0))
            def _():
                buf[c] = own[c]

        for buf, own, send, recv, side, pos, n, axis, count in flows:
            far = pos if side == 0 else n - 1 - pos
            c = s - SKEW * far

            @pl.when((c >= 0) & (c < count) & (far < n - 1))
            def _():
                hop(buf, c, send, recv, side, pos, n, axis).start()

        d = s - SKEW * (nx - 1)

        @pl.when((d >= 0) & (d < lchunks))
        def _():
            lfin[h, d] = xl[d] + xr[d] - xown[d]
            final_copy(d).start()

        e = d - SKEW

        @pl.when((e >= 0) & (e < lchunks))
        def _():
            final_copy(e).wait_recv()
            for side in range(2):
                at = pl.ds(pl.multiple_of((side * lchunks + e) * lrows, lrows), lrows)
                high, low = split(lfin[side, e])
                lhi[at, :] = high
                llo[at, :] = low

    def out_copy(b):
        return pltpu.make_async_copy(
            stage.at[b % 2],
            out.at[:, :, pl.ds(pl.multiple_of(b * WIDTH, WIDTH), WIDTH)],
            os.at[b % 2],
        )

    tile = min(256, rows)

    def compute(b):
        at = pl.ds(b * per_group, per_group)
        whole = fl[at] + fr[at] - rc[at]
        for k in range(kcount):
            slab = whole[2 * k : 2 * k + 2].reshape(2 * order, WIDTH)
            mixed = jnp.dot(amat[k], slab, precision=lax.Precision.HIGHEST, preferred_element_type=jnp.float32)
            real, imag = mixed[:order], mixed[order:]
            rest = pl.ds(k * 2 * order, order)
            more = pl.ds(k * 2 * order + order, order)
            rh, rl = split(real)
            ih, il = split(imag)
            for dst, re, im in ((bhi, rh, ih), (blo, rl, il)):
                dst[rest, :WIDTH] = re
                dst[more, :WIDTH] = -im
                dst[rest, WIDTH:] = im
                dst[more, WIDTH:] = re

        @pl.when(b >= 2)
        def _():
            out_copy(b - 2).wait()

        @pl.loop(0, rows // tile)
        def _(m):
            at = pl.ds(pl.multiple_of(m * tile, tile), tile)
            part = functools.partial(jnp.dot, preferred_element_type=jnp.float32)
            acc = part(lhi[at, :], blo[...]) + part(llo[at, :], bhi[...])
            acc = acc + part(lhi[at, :], bhi[...])
            stage[b % 2, 0, at, :] = acc[:, :WIDTH]
            stage[b % 2, 1, at, :] = acc[:, WIDTH:]

        out_copy(b).start()

    l_steps = SKEW * nx + lchunks
    first = max(l_steps, SKEW * (nz - 1) + per_group, SKEW * (nz - 1) + chunks - PACE * (groups - 1))

    @pl.loop(0, first)
    def _(s):
        step(s)

    @pl.loop(0, groups)
    def _(b):
        compute(b)

        @pl.loop(0, PACE)
        def _(i):
            step(first + PACE * b + i)

    for b in range(max(0, groups - 2), groups):
        out_copy(b).wait()

    for buf, own, send, recv, side, pos, n, axis, count in flows:
        far = pos if side == 0 else n - 1 - pos

        @pl.when(far < n - 1)
        def _():
            @pl.loop(0, count)
            def _(c):
                hop(buf, c, send, recv, side, pos, n, axis).wait_send()

    @pl.loop(0, lchunks)
    def _(c):
        half_copy(c).wait_send()
        final_copy(c).wait_send()


def insertion_matrix(op_real, op_imag, sign_row, perm_row):
    spins, vecs = sign_row.shape[0], op_real.shape[0]
    order = spins * vecs
    spread = lambda row: jnp.repeat(row, vecs, total_repeat_length=order)[:, None]
    chosen = spread(perm_row) == (lax.broadcasted_iota(jnp.int32, (order, order), 1) // vecs)
    sign = spread(sign_row)
    one = lambda value: (sign == value).astype(jnp.float32)
    phase_real = one(0) - one(2)
    phase_imag = one(1) - one(3)
    real, imag = jnp.tile(op_real, (spins, spins)), jnp.tile(op_imag, (spins, spins))
    a_real = jnp.where(chosen, phase_real * real - phase_imag * imag, 0.0)
    a_imag = jnp.where(chosen, phase_real * imag + phase_imag * real, 0.0)
    return jnp.block([[a_real, -a_imag], [a_imag, a_real]])


def shards(nz, nx, ns, perambulator, insertion_ops, ins_times, sign_table, perm_table):
    kcount, vecs = insertion_ops.shape[0], insertion_ops.shape[2]
    order = sign_table.shape[1] * vecs
    rows, cols = perambulator.shape[1:]
    piece = min(order, rows)
    times = cols // order
    z = lax.axis_index("row")
    place = lax.axis_index("col") * ns + lax.axis_index("spin")
    row_parts, col_parts, mats = [], [], []
    for k in range(kcount):
        moment = ins_times[k]
        column = lax.dynamic_slice_in_dim(perambulator, moment % times * order, order, 2)
        col_parts.append(jnp.where(place == moment // times, column, 0.0))
        pieces = []
        for index in range(order // piece):
            start = moment * order + index * piece
            found = lax.dynamic_slice_in_dim(perambulator, start % rows, piece, 1)
            pieces.append(jnp.where(z == start // rows, found, 0.0))
        row_parts.append(jnp.concatenate(pieces, axis=1))
        mats.append(insertion_matrix(insertion_ops[k, 0], insertion_ops[k, 1], sign_table[k], perm_table[k]))
    groups, per_group = cols // WIDTH, 2 * kcount
    chunks = groups * per_group
    rc = jnp.stack(row_parts).reshape(per_group, order, groups, WIDTH)
    rc = rc.transpose(2, 0, 1, 3).reshape(chunks, order, WIDTH)
    lrows = min(32, rows // 2)
    lchunks = rows // (2 * lrows)
    depth = per_group * order
    lc = jnp.concatenate([part[i] for part in col_parts for i in range(2)], axis=1)
    lc = lc.reshape(2, lchunks, lrows, depth)
    amat = jnp.stack(mats)
    sizes = (nz, nx, kcount, order, rows, groups, per_group, lchunks, lrows)
    f32, bf16, dma = jnp.float32, jnp.bfloat16, pltpu.SemaphoreType.DMA
    return pl.pallas_call(
        functools.partial(kernel, sizes),
        out_shape=jax.ShapeDtypeStruct((2, rows, cols), f32),
        in_specs=[pl.BlockSpec(memory_space=pltpu.VMEM)] * 3,
        out_specs=pl.BlockSpec(memory_space=pl.ANY),
        scratch_shapes=[
            pltpu.VMEM((chunks, order, WIDTH), f32),
            pltpu.VMEM((chunks, order, WIDTH), f32),
            pltpu.VMEM((lchunks, lrows, depth), f32),
            pltpu.VMEM((lchunks, lrows, depth), f32),
            pltpu.VMEM((lchunks, lrows, depth), f32),
            pltpu.VMEM((lchunks, lrows, depth), f32),
            pltpu.VMEM((2, lchunks, lrows, depth), f32),
            pltpu.VMEM((rows, depth), bf16),
            pltpu.VMEM((rows, depth), bf16),
            pltpu.VMEM((depth, 2 * WIDTH), bf16),
            pltpu.VMEM((depth, 2 * WIDTH), bf16),
            pltpu.VMEM((2, 2, rows, WIDTH), f32),
            dma((2, chunks)), dma((2, chunks)),
            dma((2, lchunks)), dma((2, lchunks)),
            dma((lchunks,)), dma((lchunks,)),
            dma((lchunks,)), dma((lchunks,)),
            dma((2,)),
        ],
        compiler_params=pltpu.CompilerParams(
            collective_id=0, has_side_effects=True, vmem_limit_bytes=60 * 1024 * 1024
        ),
    )(rc, lc, amat)


def solution(mesh):
    body = functools.partial(shards, mesh.shape["row"], mesh.shape["col"], mesh.shape["spin"])
    return jax.shard_map(
        body,
        mesh=mesh,
        in_specs=(P(None, ("cfg", "row"), ("col", "spin")), P(), P(), P(), P()),
        out_specs=P(None, ("cfg", "row"), ("col", "spin")),
        check_vma=False,
    )
```

```python
import functools

import jax
import jax.numpy as jnp
from jax import lax
from jax.experimental import pallas as pl
from jax.experimental.pallas import tpu as pltpu
from jax.sharding import PartitionSpec as P

MESH = pl.DeviceIdType.MESH
WIDTH = 128
SKEW = 3
PARTS = 2
PACE = 4


def split(value):
    high = value.astype(jnp.bfloat16)
    low = (value - high.astype(jnp.float32)).astype(jnp.bfloat16)
    return high, low


def dot3(a_high, a_low, b_high, b_low):
    part = functools.partial(jnp.dot, preferred_element_type=jnp.float32)
    return part(a_high, b_low) + part(a_low, b_high) + part(a_high, b_high)


def kernel(
    sizes,
    times, signs, perms, ops, source, out,
    held, fl, fr, lsend, ph, xown, xl, xr, lfin, ahi, alo, lhi, llo, bhi, blo, stage,
    zs, zr, xs, xrs, ps, pr, ls, lr, os, hs,
):
    nz, nx, ns, kcount, spins, vecs, rows, groups, lchunks, lrows = sizes
    order = spins * vecs
    cut = order // PARTS
    piece = min(cut, rows)
    per_group = 2 * kcount * PARTS
    chunks = groups * per_group
    local_times = groups * WIDTH // order
    z = lax.axis_index("row")
    x = lax.axis_index("col")
    h = lax.axis_index("spin")
    other = 1 - h
    load = pltpu.make_async_copy(source, held, hs)
    load.start()
    barrier = pltpu.get_barrier_semaphore()

    for pos, n, axis in ((z, nz, "row"), (x, nx, "col")):
        @pl.when(pos > 0)
        def _():
            pl.semaphore_signal(barrier, inc=1, device_id={axis: (pos + n - 1) % n}, device_id_type=MESH)

        @pl.when(pos < n - 1)
        def _():
            pl.semaphore_signal(barrier, inc=1, device_id={axis: (pos + 1) % n}, device_id_type=MESH)
    pl.semaphore_signal(barrier, inc=1, device_id={"spin": other}, device_id_type=MESH)
    ends = [jnp.where(pos == end, 1, 0) for pos, n in ((z, nz), (x, nx)) for end in (0, n - 1)]
    pl.semaphore_wait(barrier, 5 - sum(ends))

    def hop(buf, c, send, recv, side, pos, n, axis):
        to = (pos + 1) % n if side == 0 else (pos + n - 1) % n
        return pltpu.make_async_remote_copy(
            src_ref=buf.at[c], dst_ref=buf.at[c],
            send_sem=send.at[side, c], recv_sem=recv.at[side, c],
            device_id={axis: to}, device_id_type=MESH,
        )

    def half_copy(c):
        return pltpu.make_async_remote_copy(
            src_ref=lsend.at[c], dst_ref=ph.at[c],
            send_sem=ps.at[c], recv_sem=pr.at[c],
            device_id={"spin": other}, device_id_type=MESH,
        )

    def final_copy(c):
        return pltpu.make_async_remote_copy(
            src_ref=lfin.at[h, c], dst_ref=lfin.at[h, c],
            send_sem=ls.at[c], recv_sem=lr.at[c],
            device_id={"spin": other}, device_id_type=MESH,
        )

    def row_chunk(c):
        columns = pl.ds(pl.multiple_of(c // per_group * WIDTH, WIDTH), WIDTH)
        inner = c % per_group
        k = inner // (2 * PARTS)
        kind = inner // PARTS % 2
        part = inner % PARTS
        found = []
        for index in range(cut // piece):
            base = part * cut + index * piece
            stride, shift = (order, base) if rows >= order else (piece, 0)
            total = 0.0
            for spot in range(0, rows, stride):
                gain = jnp.where(times[k] * order + base == z * rows + spot + shift, 1.0, 0.0)
                at = pl.ds(pl.multiple_of(spot + shift, piece), piece)
                total = total + held[kind, at, columns] * gain
            found.append(total)
        return found[0] if len(found) == 1 else jnp.concatenate(found, axis=0)

    place = x * ns + h

    def column_chunk(side, c):
        at = pl.ds(pl.multiple_of((side * lchunks + c) * lrows, lrows), lrows)
        found = []
        for k in range(kcount):
            gains = [jnp.where(times[k] == place * local_times + spot, 1.0, 0.0) for spot in range(local_times)]
            for kind in range(2):
                total = 0.0
                for spot, gain in enumerate(gains):
                    total = total + held[kind, at, pl.ds(spot * order, order)] * gain
                found.append(total)
        return jnp.concatenate(found, axis=1)

    def x_own(c):
        return xown[c]

    flows = (
        (fl, row_chunk, zs, zr, 0, z, nz, "row", chunks, 0),
        (fr, row_chunk, zs, zr, 1, z, nz, "row", chunks, 0),
        (xl, x_own, xs, xrs, 0, x, nx, "col", lchunks, 1),
        (xr, x_own, xs, xrs, 1, x, nx, "col", lchunks, 1),
    )

    def build():
        lane = lax.broadcasted_iota(jnp.int32, (vecs, order), 1) // vecs
        for k in range(kcount):
            real = jnp.concatenate([ops[k, 0]] * spins, axis=1)
            imag = jnp.concatenate([ops[k, 1]] * spins, axis=1)
            for spin in range(spins):
                sign = signs[k, spin]
                phase_real = jnp.where(sign == 0, 1.0, 0.0) - jnp.where(sign == 2, 1.0, 0.0)
                phase_imag = jnp.where(sign == 1, 1.0, 0.0) - jnp.where(sign == 3, 1.0, 0.0)
                chosen = jnp.where(lane == perms[k, spin], 1.0, 0.0)
                a_real = (phase_real * real - phase_imag * imag) * chosen
                a_imag = (phase_real * imag + phase_imag * real) * chosen
                for dst, re, im in zip((ahi, alo), split(a_real), split(a_imag)):
                    top = pl.ds(spin * vecs, vecs)
                    low = pl.ds(order + spin * vecs, vecs)
                    dst[k, top, :order] = re
                    dst[k, top, order:] = -im
                    dst[k, low, :order] = im
                    dst[k, low, order:] = re

    def step(s):
        @pl.when(s < lchunks)
        def _():
            lsend[s] = column_chunk(other, s)

        @pl.when((s >= 1) & (s < lchunks + 1))
        def _():
            half_copy(s - 1).wait_recv()
            xown[s - 1] = column_chunk(h, s - 1) + ph[s - 1]

        @pl.when(s == 4)
        def _():
            build()

        for buf, own, send, recv, side, pos, n, axis, count, lag in flows:
            far = pos if side == 0 else n - 1 - pos
            c = s - SKEW * far - lag
            live = (c >= 0) & (c < count)

            @pl.when(live & (far > 0))
            def _():
                hop(buf, c, send, recv, side, pos, n, axis).wait_recv()
                buf[c] = buf[c] + own(c)

            @pl.when(live & (far == 0))
            def _():
                buf[c] = own(c)

        for buf, own, send, recv, side, pos, n, axis, count, lag in flows:
            far = pos if side == 0 else n - 1 - pos
            c = s - SKEW * far - lag

            @pl.when((c >= 0) & (c < count) & (far < n - 1))
            def _():
                hop(buf, c, send, recv, side, pos, n, axis).start()

        @pl.when(s < lchunks)
        def _():
            half_copy(s).start()

        d = s - SKEW * (nx - 1) - 1

        @pl.when((d >= 0) & (d < lchunks))
        def _():
            lfin[h, d] = xl[d] + xr[d] - xown[d]
            final_copy(d).start()

        e = d - SKEW

        @pl.when((e >= 0) & (e < lchunks))
        def _():
            final_copy(e).wait_recv()
            for side in range(2):
                at = pl.ds(pl.multiple_of((side * lchunks + e) * lrows, lrows), lrows)
                high, low = split(lfin[side, e])
                lhi[at, :] = high
                llo[at, :] = low

    def out_copy(b):
        return pltpu.make_async_copy(
            stage.at[b % 2],
            out.at[:, :, pl.ds(pl.multiple_of(b * WIDTH, WIDTH), WIDTH)],
            os.at[b % 2],
        )

    tile = min(256, rows)

    def compute(b):
        for k in range(kcount):
            found = []
            for inner in range(2 * PARTS):
                c = b * per_group + k * 2 * PARTS + inner
                found.append(fl[c] + fr[c] - row_chunk(c))
            slab_high, slab_low = split(jnp.concatenate(found, axis=0))
            mixed = dot3(ahi[k], alo[k], slab_high, slab_low)
            real, imag = mixed[:order], mixed[order:]
            rest = pl.ds(k * 2 * order, order)
            more = pl.ds(k * 2 * order + order, order)
            rh, rl = split(real)
            ih, il = split(imag)
            for dst, re, im in ((bhi, rh, ih), (blo, rl, il)):
                dst[rest, :WIDTH] = re
                dst[more, :WIDTH] = -im
                dst[rest, WIDTH:] = im
                dst[more, WIDTH:] = re

        @pl.when(b >= 2)
        def _():
            out_copy(b - 2).wait()

        @pl.loop(0, rows // tile)
        def _(m):
            at = pl.ds(pl.multiple_of(m * tile, tile), tile)
            acc = dot3(lhi[at, :], llo[at, :], bhi[...], blo[...])
            stage[b % 2, 0, at, :] = acc[:, :WIDTH]
            stage[b % 2, 1, at, :] = acc[:, WIDTH:]

        out_copy(b).start()

    l_steps = SKEW * nx + lchunks + 1
    load.wait()
    first = max(l_steps, SKEW * (nz - 1) + per_group, SKEW * (nz - 1) + chunks - PACE * (groups - 1))

    @pl.loop(0, first)
    def _(s):
        step(s)

    @pl.loop(0, groups)
    def _(b):
        compute(b)

        @pl.loop(0, PACE)
        def _(i):
            step(first + PACE * b + i)

    for b in range(max(0, groups - 2), groups):
        out_copy(b).wait()

    for buf, own, send, recv, side, pos, n, axis, count, lag in flows:
        far = pos if side == 0 else n - 1 - pos

        @pl.when(far < n - 1)
        def _():
            @pl.loop(0, count)
            def _(c):
                hop(buf, c, send, recv, side, pos, n, axis).wait_send()

    @pl.loop(0, lchunks)
    def _(c):
        half_copy(c).wait_send()
        final_copy(c).wait_send()


def shards(nz, nx, ns, perambulator, insertion_ops, ins_times, sign_table, perm_table):
    kcount, vecs, spins = insertion_ops.shape[0], insertion_ops.shape[2], sign_table.shape[1]
    order = spins * vecs
    rows, cols = perambulator.shape[1:]
    groups, cut = cols // WIDTH, order // PARTS
    chunks = groups * 2 * kcount * PARTS
    lrows = min(32 // PARTS, rows // 2)
    lchunks = rows // (2 * lrows)
    depth = 2 * kcount * order
    sizes = (nz, nx, ns, kcount, spins, vecs, rows, groups, lchunks, lrows)
    f32, bf16, dma = jnp.float32, jnp.bfloat16, pltpu.SemaphoreType.DMA
    smem, vmem = pl.BlockSpec(memory_space=pltpu.SMEM), pl.BlockSpec(memory_space=pltpu.VMEM)
    return pl.pallas_call(
        functools.partial(kernel, sizes),
        out_shape=jax.ShapeDtypeStruct((2, rows, cols), f32),
        in_specs=[smem, smem, smem, vmem, pl.BlockSpec(memory_space=pl.ANY)],
        out_specs=pl.BlockSpec(memory_space=pl.ANY),
        scratch_shapes=[
            pltpu.VMEM((2, rows, cols), f32),
            pltpu.VMEM((chunks, cut, WIDTH), f32),
            pltpu.VMEM((chunks, cut, WIDTH), f32),
            pltpu.VMEM((lchunks, lrows, depth), f32),
            pltpu.VMEM((lchunks, lrows, depth), f32),
            pltpu.VMEM((lchunks, lrows, depth), f32),
            pltpu.VMEM((lchunks, lrows, depth), f32),
            pltpu.VMEM((lchunks, lrows, depth), f32),
            pltpu.VMEM((2, lchunks, lrows, depth), f32),
            pltpu.VMEM((kcount, 2 * order, 2 * order), bf16),
            pltpu.VMEM((kcount, 2 * order, 2 * order), bf16),
            pltpu.VMEM((rows, depth), bf16),
            pltpu.VMEM((rows, depth), bf16),
            pltpu.VMEM((depth, 2 * WIDTH), bf16),
            pltpu.VMEM((depth, 2 * WIDTH), bf16),
            pltpu.VMEM((2, 2, rows, WIDTH), f32),
            dma((2, chunks)), dma((2, chunks)),
            dma((2, lchunks)), dma((2, lchunks)),
            dma((lchunks,)), dma((lchunks,)),
            dma((lchunks,)), dma((lchunks,)),
            dma((2,)), dma,
        ],
        compiler_params=pltpu.CompilerParams(
            collective_id=0, has_side_effects=True, vmem_limit_bytes=60 * 1024 * 1024
        ),
    )(ins_times, sign_table, perm_table, insertion_ops, perambulator)


def solution(mesh):
    body = functools.partial(shards, mesh.shape["row"], mesh.shape["col"], mesh.shape["spin"])
    return jax.shard_map(
        body,
        mesh=mesh,
        in_specs=(P(None, ("cfg", "row"), ("col", "spin")), P(), P(), P(), P()),
        out_specs=P(None, ("cfg", "row"), ("col", "spin")),
        check_vma=False,
    )
```

```python
import functools

import jax
import jax.numpy as jnp
from jax import lax
from jax.experimental import pallas as pl
from jax.experimental.pallas import tpu as pltpu
from jax.sharding import PartitionSpec as P

MESH = pl.DeviceIdType.MESH
WIDTH = 128
SKEW = 4
PARTS = 2
PACE = 4
LAG = 3
LOADS = 2


def split(value):
    high = value.astype(jnp.bfloat16)
    low = (value - high.astype(jnp.float32)).astype(jnp.bfloat16)
    return high, low


def dot3(a_high, a_low, b_high, b_low):
    part = functools.partial(jnp.dot, preferred_element_type=jnp.float32)
    return part(a_high, b_low) + part(a_low, b_high) + part(a_high, b_high)


def kernel(
    sizes,
    times, signs, perms, ops, source, out,
    held, fl, fr, lsend, ph, xown, xl, xr, lfin, ahi, alo, lhi, llo, bhi, blo, stage,
    zs, zr, xs, xrs, ps, pr, ls, lr, os, hs,
):
    nz, nx, ns, kcount, spins, vecs, rows, groups, lchunks, lrows = sizes
    order = spins * vecs
    cut = order // PARTS
    piece = min(cut, rows)
    per_group = 2 * kcount * PARTS
    chunks = groups * per_group
    local_times = groups * WIDTH // order
    z = lax.axis_index("row")
    x = lax.axis_index("col")
    h = lax.axis_index("spin")
    other = 1 - h
    begin = -(-groups // LOADS)

    def load(g):
        at = pl.ds(pl.multiple_of(g * WIDTH, WIDTH), WIDTH)
        return pltpu.make_async_copy(source.at[:, :, at], held.at[:, :, at], hs.at[g])

    @pl.loop(0, groups)
    def _(g):
        load(g).start()

    barrier = pltpu.get_barrier_semaphore()

    for pos, n, axis in ((z, nz, "row"), (x, nx, "col")):
        @pl.when(pos > 0)
        def _():
            pl.semaphore_signal(barrier, inc=1, device_id={axis: (pos + n - 1) % n}, device_id_type=MESH)

        @pl.when(pos < n - 1)
        def _():
            pl.semaphore_signal(barrier, inc=1, device_id={axis: (pos + 1) % n}, device_id_type=MESH)
    pl.semaphore_signal(barrier, inc=1, device_id={"spin": other}, device_id_type=MESH)
    ends = [jnp.where(pos == end, 1, 0) for pos, n in ((z, nz), (x, nx)) for end in (0, n - 1)]
    pl.semaphore_wait(barrier, 5 - sum(ends))

    def hop(buf, c, send, recv, side, pos, n, axis):
        to = (pos + 1) % n if side == 0 else (pos + n - 1) % n
        return pltpu.make_async_remote_copy(
            src_ref=buf.at[c], dst_ref=buf.at[c],
            send_sem=send.at[side, c], recv_sem=recv.at[side, c],
            device_id={axis: to}, device_id_type=MESH,
        )

    def half_copy(c):
        return pltpu.make_async_remote_copy(
            src_ref=lsend.at[c], dst_ref=ph.at[c],
            send_sem=ps.at[c], recv_sem=pr.at[c],
            device_id={"spin": other}, device_id_type=MESH,
        )

    def final_copy(c):
        return pltpu.make_async_remote_copy(
            src_ref=lfin.at[h, c], dst_ref=lfin.at[h, c],
            send_sem=ls.at[c], recv_sem=lr.at[c],
            device_id={"spin": other}, device_id_type=MESH,
        )

    def row_chunk(c):
        columns = pl.ds(pl.multiple_of(c // per_group * WIDTH, WIDTH), WIDTH)
        inner = c % per_group
        k = inner // (2 * PARTS)
        kind = inner // PARTS % 2
        part = inner % PARTS
        found = []
        for index in range(cut // piece):
            base = part * cut + index * piece
            stride, shift = (order, base) if rows >= order else (piece, 0)
            total = 0.0
            for spot in range(0, rows, stride):
                gain = jnp.where(times[k] * order + base == z * rows + spot + shift, 1.0, 0.0)
                at = pl.ds(pl.multiple_of(spot + shift, piece), piece)
                total = total + held[kind, at, columns] * gain
            found.append(total)
        return found[0] if len(found) == 1 else jnp.concatenate(found, axis=0)

    place = x * ns + h

    def column_chunk(side, c):
        at = pl.ds(pl.multiple_of((side * lchunks + c) * lrows, lrows), lrows)
        found = []
        for k in range(kcount):
            gains = [jnp.where(times[k] == place * local_times + spot, 1.0, 0.0) for spot in range(local_times)]
            for kind in range(2):
                total = 0.0
                for spot, gain in enumerate(gains):
                    total = total + held[kind, at, pl.ds(spot * order, order)] * gain
                found.append(total)
        return jnp.concatenate(found, axis=1)

    def x_own(c):
        return xown[c]

    flows = (
        (fl, row_chunk, zs, zr, 0, z, nz, "row", chunks, 0),
        (fr, row_chunk, zs, zr, 1, z, nz, "row", chunks, 0),
        (xl, x_own, xs, xrs, 0, x, nx, "col", lchunks, begin + LAG),
        (xr, x_own, xs, xrs, 1, x, nx, "col", lchunks, begin + LAG),
    )

    def build():
        lane = lax.broadcasted_iota(jnp.int32, (vecs, order), 1) // vecs
        for k in range(kcount):
            real = jnp.concatenate([ops[k, 0]] * spins, axis=1)
            imag = jnp.concatenate([ops[k, 1]] * spins, axis=1)
            for spin in range(spins):
                sign = signs[k, spin]
                phase_real = jnp.where(sign == 0, 1.0, 0.0) - jnp.where(sign == 2, 1.0, 0.0)
                phase_imag = jnp.where(sign == 1, 1.0, 0.0) - jnp.where(sign == 3, 1.0, 0.0)
                chosen = jnp.where(lane == perms[k, spin], 1.0, 0.0)
                a_real = (phase_real * real - phase_imag * imag) * chosen
                a_imag = (phase_real * imag + phase_imag * real) * chosen
                for dst, re, im in zip((ahi, alo), split(a_real), split(a_imag)):
                    top = pl.ds(spin * vecs, vecs)
                    low = pl.ds(order + spin * vecs, vecs)
                    dst[k, top, :order] = re
                    dst[k, top, order:] = -im
                    dst[k, low, :order] = im
                    dst[k, low, order:] = re

    def step(s):
        @pl.when(s < begin)
        def _():
            for i in range(LOADS):
                @pl.when(s * LOADS + i < groups)
                def _():
                    load(s * LOADS + i).wait()

        f = s - begin

        @pl.when((f >= 0) & (f < lchunks))
        def _():
            lsend[f] = column_chunk(other, f)

        a = f - LAG

        @pl.when((a >= 0) & (a < lchunks))
        def _():
            half_copy(a).wait_recv()
            xown[a] = column_chunk(h, a) + ph[a]

        @pl.when(s == 4)
        def _():
            build()

        for buf, own, send, recv, side, pos, n, axis, count, lag in flows:
            far = pos if side == 0 else n - 1 - pos
            c = s - SKEW * far - lag
            live = (c >= 0) & (c < count)

            @pl.when(live & (far > 0))
            def _():
                hop(buf, c, send, recv, side, pos, n, axis).wait_recv()
                buf[c] = buf[c] + own(c)

            @pl.when(live & (far == 0))
            def _():
                buf[c] = own(c)

        for buf, own, send, recv, side, pos, n, axis, count, lag in flows:
            far = pos if side == 0 else n - 1 - pos
            c = s - SKEW * far - lag

            @pl.when((c >= 0) & (c < count) & (far < n - 1))
            def _():
                hop(buf, c, send, recv, side, pos, n, axis).start()

        @pl.when((f >= 0) & (f < lchunks))
        def _():
            half_copy(f).start()

        d = f - SKEW * (nx - 1) - LAG

        @pl.when((d >= 0) & (d < lchunks))
        def _():
            lfin[h, d] = xl[d] + xr[d] - xown[d]
            final_copy(d).start()

        e = d - SKEW

        @pl.when((e >= 0) & (e < lchunks))
        def _():
            final_copy(e).wait_recv()
            for side in range(2):
                at = pl.ds(pl.multiple_of((side * lchunks + e) * lrows, lrows), lrows)
                high, low = split(lfin[side, e])
                lhi[at, :] = high
                llo[at, :] = low

    def out_copy(b):
        return pltpu.make_async_copy(
            stage.at[b % 2],
            out.at[:, :, pl.ds(pl.multiple_of(b * WIDTH, WIDTH), WIDTH)],
            os.at[b % 2],
        )

    tile = rows // PACE

    def mix(b):
        for k in range(kcount):
            found = []
            for inner in range(2 * PARTS):
                c = b * per_group + k * 2 * PARTS + inner
                found.append(fl[c] + fr[c] - row_chunk(c))
            slab_high, slab_low = split(jnp.concatenate(found, axis=0))
            mixed = dot3(ahi[k], alo[k], slab_high, slab_low)
            real, imag = mixed[:order], mixed[order:]
            rest = pl.ds(k * 2 * order, order)
            more = pl.ds(k * 2 * order + order, order)
            rh, rl = split(real)
            ih, il = split(imag)
            for dst, re, im in ((bhi, rh, ih), (blo, rl, il)):
                dst[rest, :WIDTH] = re
                dst[more, :WIDTH] = -im
                dst[rest, WIDTH:] = im
                dst[more, WIDTH:] = re

        @pl.when(b >= 2)
        def _():
            out_copy(b - 2).wait()

    def multiply(b, i):
        at = pl.ds(pl.multiple_of(i * tile, tile), tile)
        acc = dot3(lhi[at, :], llo[at, :], bhi[...], blo[...])
        stage[b % 2, 0, at, :] = acc[:, :WIDTH]
        stage[b % 2, 1, at, :] = acc[:, WIDTH:]

    l_steps = SKEW * nx + lchunks + LAG + begin
    first = max(l_steps, SKEW * (nz - 1) + per_group, SKEW * (nz - 1) + chunks - PACE * (groups - 1))

    @pl.loop(0, first)
    def _(s):
        step(s)

    @pl.loop(0, groups)
    def _(b):
        mix(b)

        @pl.loop(0, PACE)
        def _(i):
            multiply(b, i)
            step(first + PACE * b + i)

        out_copy(b).start()

    for b in range(max(0, groups - 2), groups):
        out_copy(b).wait()

    for buf, own, send, recv, side, pos, n, axis, count, lag in flows:
        far = pos if side == 0 else n - 1 - pos

        @pl.when(far < n - 1)
        def _():
            @pl.loop(0, count)
            def _(c):
                hop(buf, c, send, recv, side, pos, n, axis).wait_send()

    @pl.loop(0, lchunks)
    def _(c):
        half_copy(c).wait_send()
        final_copy(c).wait_send()


def shards(nz, nx, ns, perambulator, insertion_ops, ins_times, sign_table, perm_table):
    kcount, vecs, spins = insertion_ops.shape[0], insertion_ops.shape[2], sign_table.shape[1]
    order = spins * vecs
    rows, cols = perambulator.shape[1:]
    groups, cut = cols // WIDTH, order // PARTS
    chunks = groups * 2 * kcount * PARTS
    lrows = min(32 // PARTS, rows // 2)
    lchunks = rows // (2 * lrows)
    depth = 2 * kcount * order
    sizes = (nz, nx, ns, kcount, spins, vecs, rows, groups, lchunks, lrows)
    f32, bf16, dma = jnp.float32, jnp.bfloat16, pltpu.SemaphoreType.DMA
    smem, vmem = pl.BlockSpec(memory_space=pltpu.SMEM), pl.BlockSpec(memory_space=pltpu.VMEM)
    return pl.pallas_call(
        functools.partial(kernel, sizes),
        out_shape=jax.ShapeDtypeStruct((2, rows, cols), f32),
        in_specs=[smem, smem, smem, vmem, pl.BlockSpec(memory_space=pl.ANY)],
        out_specs=pl.BlockSpec(memory_space=pl.ANY),
        scratch_shapes=[
            pltpu.VMEM((2, rows, cols), f32),
            pltpu.VMEM((chunks, cut, WIDTH), f32),
            pltpu.VMEM((chunks, cut, WIDTH), f32),
            pltpu.VMEM((lchunks, lrows, depth), f32),
            pltpu.VMEM((lchunks, lrows, depth), f32),
            pltpu.VMEM((lchunks, lrows, depth), f32),
            pltpu.VMEM((lchunks, lrows, depth), f32),
            pltpu.VMEM((lchunks, lrows, depth), f32),
            pltpu.VMEM((2, lchunks, lrows, depth), f32),
            pltpu.VMEM((kcount, 2 * order, 2 * order), bf16),
            pltpu.VMEM((kcount, 2 * order, 2 * order), bf16),
            pltpu.VMEM((rows, depth), bf16),
            pltpu.VMEM((rows, depth), bf16),
            pltpu.VMEM((depth, 2 * WIDTH), bf16),
            pltpu.VMEM((depth, 2 * WIDTH), bf16),
            pltpu.VMEM((2, 2, rows, WIDTH), f32),
            dma((2, chunks)), dma((2, chunks)),
            dma((2, lchunks)), dma((2, lchunks)),
            dma((lchunks,)), dma((lchunks,)),
            dma((lchunks,)), dma((lchunks,)),
            dma((2,)), dma((groups,)),
        ],
        compiler_params=pltpu.CompilerParams(
            collective_id=0, has_side_effects=True, vmem_limit_bytes=44 * 1024 * 1024
        ),
    )(ins_times, sign_table, perm_table, insertion_ops, perambulator)


def solution(mesh):
    body = functools.partial(shards, mesh.shape["row"], mesh.shape["col"], mesh.shape["spin"])
    return jax.shard_map(
        body,
        mesh=mesh,
        in_specs=(P(None, ("cfg", "row"), ("col", "spin")), P(), P(), P(), P()),
        out_specs=P(None, ("cfg", "row"), ("col", "spin")),
        check_vma=False,
    )
```

```python
import functools

import jax
import jax.numpy as jnp
from jax import lax
from jax.experimental import pallas as pl
from jax.experimental.pallas import tpu as pltpu
from jax.sharding import PartitionSpec as P

MESH = pl.DeviceIdType.MESH
WIDTH = 128
SKEW = 4
PARTS = 2
PACE = 4
TILES = 2
LAG = 3
LOADS = 2


def split(value):
    high = value.astype(jnp.bfloat16)
    low = (value - high.astype(jnp.float32)).astype(jnp.bfloat16)
    return high, low


def dot3(a_high, a_low, b_high, b_low):
    part = functools.partial(jnp.dot, preferred_element_type=jnp.float32)
    return part(a_high, b_low) + part(a_low, b_high) + part(a_high, b_high)


def kernel(
    sizes,
    table, ops, source, out,
    held, fl, fr, lsend, ph, xown, xl, xr, lfin, ahi, alo, lhi, llo, bhi, blo, stage,
    zs, zr, xs, xrs, ps, pr, ls, lr, os, hs,
):
    nz, nx, ns, kcount, spins, vecs, rows, groups, lchunks, lrows = sizes
    order = spins * vecs
    cut = order // PARTS
    piece = min(cut, rows)
    per_group = 2 * kcount * PARTS
    chunks = groups * per_group
    local_times = groups * WIDTH // order
    z = lax.axis_index("row")
    x = lax.axis_index("col")
    h = lax.axis_index("spin")
    other = 1 - h
    begin = -(-groups // LOADS)

    def load(g):
        at = pl.ds(pl.multiple_of(g * WIDTH, WIDTH), WIDTH)
        return pltpu.make_async_copy(source.at[:, :, at], held.at[:, :, at], hs.at[g])

    @pl.loop(0, groups)
    def _(g):
        load(g).start()

    barrier = pltpu.get_barrier_semaphore()

    for pos, n, axis in ((z, nz, "row"), (x, nx, "col")):
        @pl.when(pos > 0)
        def _():
            pl.semaphore_signal(barrier, inc=1, device_id={axis: (pos + n - 1) % n}, device_id_type=MESH)

        @pl.when(pos < n - 1)
        def _():
            pl.semaphore_signal(barrier, inc=1, device_id={axis: (pos + 1) % n}, device_id_type=MESH)
    pl.semaphore_signal(barrier, inc=1, device_id={"spin": other}, device_id_type=MESH)
    ends = [jnp.where(pos == end, 1, 0) for pos, n in ((z, nz), (x, nx)) for end in (0, n - 1)]
    pl.semaphore_wait(barrier, 5 - sum(ends))

    def hop(buf, c, send, recv, side, pos, n, axis):
        to = (pos + 1) % n if side == 0 else (pos + n - 1) % n
        return pltpu.make_async_remote_copy(
            src_ref=buf.at[c], dst_ref=buf.at[c],
            send_sem=send.at[side, c], recv_sem=recv.at[side, c],
            device_id={axis: to}, device_id_type=MESH,
        )

    def half_copy(c):
        return pltpu.make_async_remote_copy(
            src_ref=lsend.at[c], dst_ref=ph.at[c],
            send_sem=ps.at[c], recv_sem=pr.at[c],
            device_id={"spin": other}, device_id_type=MESH,
        )

    def final_copy(c):
        return pltpu.make_async_remote_copy(
            src_ref=lfin.at[h, c], dst_ref=lfin.at[h, c],
            send_sem=ls.at[c], recv_sem=lr.at[c],
            device_id={"spin": other}, device_id_type=MESH,
        )

    def row_chunk(c):
        columns = pl.ds(pl.multiple_of(c // per_group * WIDTH, WIDTH), WIDTH)
        inner = c % per_group
        k = inner // (2 * PARTS)
        kind = inner // PARTS % 2
        part = inner % PARTS
        found = []
        for index in range(cut // piece):
            base = part * cut + index * piece
            stride, shift = (order, base) if rows >= order else (piece, 0)
            total = 0.0
            for spot in range(0, rows, stride):
                gain = jnp.where(table[k, 0] * order + base == z * rows + spot + shift, 1.0, 0.0)
                at = pl.ds(pl.multiple_of(spot + shift, piece), piece)
                total = total + held[kind, at, columns] * gain
            found.append(total)
        return found[0] if len(found) == 1 else jnp.concatenate(found, axis=0)

    place = x * ns + h

    def column_chunk(side, c):
        at = pl.ds(pl.multiple_of((side * lchunks + c) * lrows, lrows), lrows)
        found = []
        for k in range(kcount):
            gains = [jnp.where(table[k, 0] == place * local_times + spot, 1.0, 0.0) for spot in range(local_times)]
            for kind in range(2):
                total = 0.0
                for spot, gain in enumerate(gains):
                    total = total + held[kind, at, pl.ds(spot * order, order)] * gain
                found.append(total)
        return jnp.concatenate(found, axis=1)

    def x_own(c):
        return xown[c]

    flows = (
        (fl, row_chunk, zs, zr, 0, z, nz, "row", chunks, 0),
        (fr, row_chunk, zs, zr, 1, z, nz, "row", chunks, 0),
        (xl, x_own, xs, xrs, 0, x, nx, "col", lchunks, begin + LAG),
        (xr, x_own, xs, xrs, 1, x, nx, "col", lchunks, begin + LAG),
    )

    def build():
        lane = lax.broadcasted_iota(jnp.int32, (vecs, order), 1) // vecs
        for k in range(kcount):
            real = jnp.concatenate([ops[k, 0]] * spins, axis=1)
            imag = jnp.concatenate([ops[k, 1]] * spins, axis=1)
            for spin in range(spins):
                sign = table[k, 1 + spin]
                phase_real = jnp.where(sign == 0, 1.0, 0.0) - jnp.where(sign == 2, 1.0, 0.0)
                phase_imag = jnp.where(sign == 1, 1.0, 0.0) - jnp.where(sign == 3, 1.0, 0.0)
                chosen = jnp.where(lane == table[k, 1 + spins + spin], 1.0, 0.0)
                a_real = (phase_real * real - phase_imag * imag) * chosen
                a_imag = (phase_real * imag + phase_imag * real) * chosen
                for dst, re, im in zip((ahi, alo), split(a_real), split(a_imag)):
                    top = pl.ds(spin * vecs, vecs)
                    low = pl.ds(order + spin * vecs, vecs)
                    dst[k, top, :order] = re
                    dst[k, top, order:] = -im
                    dst[k, low, :order] = im
                    dst[k, low, order:] = re

    def step(s):
        @pl.when(s < begin)
        def _():
            for i in range(LOADS):
                @pl.when(s * LOADS + i < groups)
                def _():
                    load(s * LOADS + i).wait()

        f = s - begin

        @pl.when((f >= 0) & (f < lchunks))
        def _():
            lsend[f] = column_chunk(other, f)

        a = f - LAG

        @pl.when((a >= 0) & (a < lchunks))
        def _():
            half_copy(a).wait_recv()
            xown[a] = column_chunk(h, a) + ph[a]

        @pl.when(s == 4)
        def _():
            build()

        for buf, own, send, recv, side, pos, n, axis, count, lag in flows:
            far = pos if side == 0 else n - 1 - pos
            c = s - SKEW * far - lag
            live = (c >= 0) & (c < count)

            @pl.when(live & (far > 0))
            def _():
                hop(buf, c, send, recv, side, pos, n, axis).wait_recv()
                buf[c] = buf[c] + own(c)

            @pl.when(live & (far == 0))
            def _():
                buf[c] = own(c)

        for buf, own, send, recv, side, pos, n, axis, count, lag in flows:
            far = pos if side == 0 else n - 1 - pos
            c = s - SKEW * far - lag

            @pl.when((c >= 0) & (c < count) & (far < n - 1))
            def _():
                hop(buf, c, send, recv, side, pos, n, axis).start()

        @pl.when((f >= 0) & (f < lchunks))
        def _():
            half_copy(f).start()

        d = f - SKEW * (nx - 1) - LAG

        @pl.when((d >= 0) & (d < lchunks))
        def _():
            lfin[h, d] = xl[d] + xr[d] - xown[d]
            final_copy(d).start()

        e = d - SKEW

        @pl.when((e >= 0) & (e < lchunks))
        def _():
            final_copy(e).wait_recv()
            for side in range(2):
                at = pl.ds(pl.multiple_of((side * lchunks + e) * lrows, lrows), lrows)
                high, low = split(lfin[side, e])
                lhi[at, :] = high
                llo[at, :] = low

    def out_copy(b):
        return pltpu.make_async_copy(
            stage.at[b % 2],
            out.at[:, :, pl.ds(pl.multiple_of(b * WIDTH, WIDTH), WIDTH)],
            os.at[b % 2],
        )

    tile = rows // TILES
    each = PACE // TILES

    def mix(b):
        for k in range(kcount):
            found = []
            for inner in range(2 * PARTS):
                c = b * per_group + k * 2 * PARTS + inner
                found.append(fl[c] + fr[c] - row_chunk(c))
            slab_high, slab_low = split(jnp.concatenate(found, axis=0))
            mixed = dot3(ahi[k], alo[k], slab_high, slab_low)
            real, imag = mixed[:order], mixed[order:]
            rest = pl.ds(k * 2 * order, order)
            more = pl.ds(k * 2 * order + order, order)
            rh, rl = split(real)
            ih, il = split(imag)
            for dst, re, im in ((bhi, rh, ih), (blo, rl, il)):
                dst[rest, :WIDTH] = re
                dst[more, :WIDTH] = -im
                dst[rest, WIDTH:] = im
                dst[more, WIDTH:] = re

        @pl.when(b >= 2)
        def _():
            out_copy(b - 2).wait()

    def multiply(b, i):
        at = pl.ds(pl.multiple_of(i * tile, tile), tile)
        acc = dot3(lhi[at, :], llo[at, :], bhi[...], blo[...])
        stage[b % 2, 0, at, :] = acc[:, :WIDTH]
        stage[b % 2, 1, at, :] = acc[:, WIDTH:]

    l_steps = SKEW * nx + lchunks + LAG + begin
    first = max(l_steps, SKEW * (nz - 1) + per_group, SKEW * (nz - 1) + chunks - PACE * (groups - 1))

    @pl.loop(0, first)
    def _(s):
        step(s)

    @pl.loop(0, groups)
    def _(b):
        mix(b)

        @pl.loop(0, PACE)
        def _(i):
            @pl.when(i % each == 0)
            def _():
                multiply(b, i // each)

            step(first + PACE * b + i)

        out_copy(b).start()

    for b in range(max(0, groups - 2), groups):
        out_copy(b).wait()

    for buf, own, send, recv, side, pos, n, axis, count, lag in flows:
        far = pos if side == 0 else n - 1 - pos

        @pl.when(far < n - 1)
        def _():
            @pl.loop(0, count)
            def _(c):
                hop(buf, c, send, recv, side, pos, n, axis).wait_send()

    @pl.loop(0, lchunks)
    def _(c):
        half_copy(c).wait_send()
        final_copy(c).wait_send()


def shards(nz, nx, ns, perambulator, insertion_ops, ins_times, sign_table, perm_table):
    kcount, vecs, spins = insertion_ops.shape[0], insertion_ops.shape[2], sign_table.shape[1]
    order = spins * vecs
    rows, cols = perambulator.shape[1:]
    groups, cut = cols // WIDTH, order // PARTS
    chunks = groups * 2 * kcount * PARTS
    lrows = min(32 // PARTS, rows // 2)
    lchunks = rows // (2 * lrows)
    depth = 2 * kcount * order
    sizes = (nz, nx, ns, kcount, spins, vecs, rows, groups, lchunks, lrows)
    f32, bf16, dma = jnp.float32, jnp.bfloat16, pltpu.SemaphoreType.DMA
    smem, vmem = pl.BlockSpec(memory_space=pltpu.SMEM), pl.BlockSpec(memory_space=pltpu.VMEM)
    table = jnp.concatenate([ins_times[:, None], sign_table, perm_table], axis=1)
    return pl.pallas_call(
        functools.partial(kernel, sizes),
        out_shape=jax.ShapeDtypeStruct((2, rows, cols), f32),
        in_specs=[smem, vmem, pl.BlockSpec(memory_space=pl.ANY)],
        out_specs=pl.BlockSpec(memory_space=pl.ANY),
        scratch_shapes=[
            pltpu.VMEM((2, rows, cols), f32),
            pltpu.VMEM((chunks, cut, WIDTH), f32),
            pltpu.VMEM((chunks, cut, WIDTH), f32),
            pltpu.VMEM((lchunks, lrows, depth), f32),
            pltpu.VMEM((lchunks, lrows, depth), f32),
            pltpu.VMEM((lchunks, lrows, depth), f32),
            pltpu.VMEM((lchunks, lrows, depth), f32),
            pltpu.VMEM((lchunks, lrows, depth), f32),
            pltpu.VMEM((2, lchunks, lrows, depth), f32),
            pltpu.VMEM((kcount, 2 * order, 2 * order), bf16),
            pltpu.VMEM((kcount, 2 * order, 2 * order), bf16),
            pltpu.VMEM((rows, depth), bf16),
            pltpu.VMEM((rows, depth), bf16),
            pltpu.VMEM((depth, 2 * WIDTH), bf16),
            pltpu.VMEM((depth, 2 * WIDTH), bf16),
            pltpu.VMEM((2, 2, rows, WIDTH), f32),
            dma((2, chunks)), dma((2, chunks)),
            dma((2, lchunks)), dma((2, lchunks)),
            dma((lchunks,)), dma((lchunks,)),
            dma((lchunks,)), dma((lchunks,)),
            dma((2,)), dma((groups,)),
        ],
        compiler_params=pltpu.CompilerParams(
            collective_id=0, has_side_effects=True, vmem_limit_bytes=44 * 1024 * 1024
        ),
    )(table, insertion_ops, perambulator)


def solution(mesh):
    body = functools.partial(shards, mesh.shape["row"], mesh.shape["col"], mesh.shape["spin"])
    return jax.shard_map(
        body,
        mesh=mesh,
        in_specs=(P(None, ("cfg", "row"), ("col", "spin")), P(), P(), P(), P()),
        out_specs=P(None, ("cfg", "row"), ("col", "spin")),
        check_vma=False,
    )
```
